32 devices in a mesh: expert: 16 (over z, x, core), dp: 2 (over y).
Axes of the slice: x: 2, y: 2, z: 4, core: 2. Of those that a mesh axis runs over, the one named last changes fastest.
Arguments:
- tokens: bfloat16 [1536, 2880], P(('expert', 'dp')), may hold values from -6 to 6
- expert_ids: int32 [1536, 4], P(('expert', 'dp')), may hold values from 0 to 15, all different within a row; in each aligned block of 48 rows (0 to 47, 48 to 95, ...) at most 24 rows name the same one
- combine_int: int32 [1536, 4], P(('expert', 'dp')), may hold values from 8 to 63
- gate_weight: bfloat16 [16, 2880, 2880], P('expert', None, 'dp'), may hold values from -0.109375 to 0.109375
- up_weight: bfloat16 [16, 2880, 2880], P('expert', None, 'dp'), may hold values from -0.109375 to 0.109375
- down_weight: bfloat16 [16, 2880, 2880], P('expert', 'dp'), may hold values from -0.109375 to 0.109375
Outputs:
- mixed: bfloat16 [1536, 2880], P(('expert', 'dp'))
The draws below stay inside these ranges and needn't reach their ends.
Inputs may be any that keep to these rules, and one draw needn't show every extreme that they name: `expert_ids`: each row names 4 different experts; within the 48 rows of one device no expert is named by more than 24 rows, a bound that some block reaches.
All inputs are finite; a program needn't handle non-finite values.
Results may differ from the reference program's by a relative error of at most 0.0049.
Values may be sent and summed in bfloat16 or wider, within the bound.
A program may use at most 128 MiB of HBM per device.

```python
import math
import jax
import jax.numpy as jnp
import numpy as np
from jax import lax

D = 2880
FF = 2880
TOP = 4
TOK_DEV = 48
EXPERTS = 16
CAP = 24
TOKENS = 1536


def touch_ends(drawn, key, least, top_value):
    extent = drawn.shape
    place = [jax.random.randint(jax.random.fold_in(key, axis), (), 0, extent[axis]) for axis in range(len(extent))]
    drawn = drawn.at[tuple(place)].set(least)
    longest = extent.index(max(extent))
    place[longest] = (place[longest] + 1) % extent[longest]
    return drawn.at[tuple(place)].set(top_value)


def steps_of(key, shape, cuts, low, largest):
    gain = 1.0
    for dim, blocks in cuts:
        draws = jax.random.uniform(jax.random.fold_in(jax.random.fold_in(key, 6), dim), (blocks,), jnp.float32, low / len(cuts), largest / len(cuts))
        gain = gain * jnp.repeat(jnp.exp(draws), shape[dim] // blocks).reshape((-1,) + (1,) * (len(shape) - 1 - dim))
    return gain


def deal_out(own_key, own, number, rows, amount, top, bound, lean):
    ranking = jax.random.permutation(own_key, amount)
    crowded, common = portions_of(amount, rows * top, bound, lean, True), portions_of(amount, rows * top, bound, lean, False)
    places = jnp.arange(amount)

    def named(tallies, offset_by):
        used = int((tallies > 0).sum())
        fixed = max(1, used // 4)
        passed = fixed + (places - fixed + offset_by * (used - fixed)) % max(1, amount - fixed)
        return jnp.zeros((amount,), jnp.int32).at[ranking[jnp.where(places < fixed, places, passed)]].set(jnp.asarray(tallies, jnp.int32))

    tallies = jnp.where(number % 4 == 0, named(crowded, number // 4), named(common, number - number // 4 - 1))
    mixed = jax.random.permutation(jax.random.fold_in(own, 3), amount)
    source_of, sink = mixed[0:amount // 2 * 2:2], mixed[1:amount // 2 * 2:2]
    margin = jnp.minimum(tallies[source_of] - 1, bound - tallies[sink]) // 2
    margin = jnp.where((source_of == ranking[0]) | (sink == ranking[0]) | (tallies[sink] == 0), 0, jnp.maximum(margin, 0))
    passed = jax.random.randint(jax.random.fold_in(own, 4), (amount // 2,), 0, 1 << 20) % (margin + 1)
    tallies = tallies.at[source_of].add(-passed).at[sink].add(passed)
    labels = jnp.searchsorted(jnp.cumsum(tallies), jnp.arange(rows * top), side="right").astype(jnp.int32)
    table = labels.reshape(top, rows).T
    table = table[jax.random.permutation(jax.random.fold_in(own, 1), rows)]
    offset_by = jax.random.randint(jax.random.fold_in(own, 2), (rows, 1), 0, top)
    return jnp.take_along_axis(table, (jnp.arange(top)[None, :] + offset_by) % top, axis=1)


def portions_of(amount, total, bound, slope, full):
    weights = [(1 << 20) // math.isqrt(standing ** slope) + 1 for standing in range(1, amount + 1)]
    largest = bound if full else min(bound, max(-(-total // amount), total * weights[0] // sum(weights)))
    least = 1 if total - largest >= amount - 1 else 0
    counts, rest = [largest] + [least] * (amount - 1), total - largest - least * (amount - 1)
    while rest > 0:
        free = [i for i in range(1, amount) if counts[i] < largest] or [i for i in range(1, amount) if counts[i] < bound]
        whole, budget = sum([weights[i] for i in free]), rest
        for i in free:
            extra = min(bound - counts[i], max(1, budget * weights[i] // whole), rest)
            counts[i] = counts[i] + extra
            rest = rest - extra
    return np.array(counts)


def normal_values(key, extent, scale, limit, pieces=(), kind=jnp.bfloat16):
    drawn = scale * jax.random.normal(key, extent, jnp.float32)
    if pieces:
        drawn = drawn * steps_of(key, extent, pieces, -0.22, 0.18)
    return jnp.clip(drawn, -limit, limit).astype(kind)


def setup_inputs(seed: int = 0) -> dict:
    key_list = jax.random.split(jax.random.key(seed), 7)
    tokens = normal_values(key_list[0], (TOKENS, D), 1.0, 6.0, ((0, 32),))
    expert_ids_keys = jax.random.split(jax.random.fold_in(key_list[1], 1), TOKENS // TOK_DEV)
    expert_ids_turns = jax.random.permutation(jax.random.fold_in(key_list[1], 3), TOKENS // TOK_DEV)
    expert_ids = jax.vmap(lambda own, number: deal_out(jax.random.fold_in(key_list[1], 2), own, number, TOK_DEV, EXPERTS, TOP, CAP, 2))(expert_ids_keys, expert_ids_turns).reshape((TOKENS, TOP))
    combine_int = touch_ends(jax.random.randint(key_list[2], (TOKENS, TOP), 8, 64), jax.random.fold_in(key_list[2], 1), 8, 63).astype(jnp.int32)
    gate_weight = normal_values(key_list[3], (EXPERTS, D, FF), D ** -0.5, 0.109375, ((0, 16), (2, 2)))
    up_weight = normal_values(key_list[4], (EXPERTS, D, FF), D ** -0.5, 0.109375, ((0, 16), (2, 2)))
    down_weight = normal_values(key_list[5], (EXPERTS, FF, D), FF ** -0.5, 0.109375, ((0, 16), (1, 2)))
    return {"tokens": tokens, "expert_ids": expert_ids, "combine_int": combine_int, "gate_weight": gate_weight, "up_weight": up_weight, "down_weight": down_weight}


def expert_rows(rows, gate_w, up_w, down_w):
    gate = jnp.dot(rows, gate_w, preferred_element_type=jnp.float32)
    up = jnp.dot(rows, up_w, preferred_element_type=jnp.float32)
    hidden = (gate * jax.nn.sigmoid(1.702 * gate) * (up + 1.0)).astype(jnp.bfloat16)
    return jnp.dot(hidden, down_w, preferred_element_type=jnp.float32)


def reference(tokens, expert_ids, combine_int, gate_weight, up_weight, down_weight):
    devices = TOKENS // TOK_DEV
    slots = devices * CAP
    weights = combine_int.astype(jnp.float32) / 32.0

    def one_expert(carry, index):
        hit = expert_ids == index
        chosen = jnp.any(hit, axis=1).astype(jnp.int32)
        scale = jnp.sum(jnp.where(hit, weights, jnp.zeros_like(weights)), axis=1)
        rank = jnp.cumsum(chosen.reshape(devices, TOK_DEV), axis=1) - 1
        places = (jnp.arange(devices, dtype=jnp.int32)[:, None] * CAP + rank).reshape(-1).astype(jnp.int32)
        places = jnp.where(chosen > 0, places, slots).astype(jnp.int32)
        rows = jnp.zeros((slots + 1, D), jnp.bfloat16).at[places].set(tokens)
        result = expert_rows(rows[:slots], gate_weight[index], up_weight[index], down_weight[index])
        picked = jnp.take(result, jnp.minimum(places, slots - 1), axis=0)
        return carry + scale[:, None] * picked, None

    start = jnp.zeros((TOKENS, D), jnp.float32)
    total, _ = lax.scan(one_expert, start, jnp.arange(EXPERTS, dtype=jnp.int32))
    return total.astype(jnp.bfloat16)
```

```python
import functools

import jax
import jax.numpy as jnp
from jax import lax
from jax.experimental import pallas as pl
from jax.experimental.pallas import tpu as pltpu
from jax.sharding import PartitionSpec as P

MESH = pl.DeviceIdType.MESH
BF16 = jnp.bfloat16
F32 = jnp.float32


def expert_rows(rows, gate_w, up_w, down_w):
    gate = jnp.dot(rows, gate_w, preferred_element_type=jnp.float32)
    up = jnp.dot(rows, up_w, preferred_element_type=jnp.float32)
    hidden = (gate * jax.nn.sigmoid(1.702 * gate) * (up + 1.0)).astype(jnp.bfloat16)
    return jnp.dot(hidden, down_w, preferred_element_type=jnp.float32)


def build_tables(tokens, expert_ids, combine_int, experts, capacity):
    tok_rows, top = expert_ids.shape
    flat_ids = expert_ids.reshape(-1)
    onehot = (flat_ids[:, None] == jnp.arange(experts, dtype=jnp.int32)[None, :]).astype(jnp.int32)
    ranks = jnp.sum(onehot * (jnp.cumsum(onehot, axis=0) - 1), axis=1)
    places = (flat_ids * capacity + ranks).reshape(tok_rows, top)
    slot_ids = jnp.arange(experts * capacity, dtype=jnp.int32)
    matches = places[:, :, None] == slot_ids[None, None, :]
    sender = jnp.any(matches, axis=1).astype(jnp.bfloat16)
    buffer = jnp.dot(sender.T, tokens, preferred_element_type=jnp.float32).astype(jnp.bfloat16)
    weights = combine_int.astype(jnp.float32) / 32.0
    mixing = jnp.sum(jnp.where(matches, weights[:, :, None], 0.0), axis=1)
    return (buffer.reshape(experts, capacity, tokens.shape[1]), mixing)


def padded_plan(tokens, expert_ids, combine_int, gate_weight, up_weight, down_weight):
    experts = lax.axis_size("expert")
    width = tokens.shape[1]
    capacity = 2 * expert_ids.shape[1] * tokens.shape[0] // experts
    gate_w, up_w, down_w = (gate_weight[0], up_weight[0], down_weight[0])
    buffer, mixing = build_tables(tokens, expert_ids, combine_int, experts, capacity)
    received = lax.all_to_all(buffer, "expert", split_axis=0, concat_axis=0, tiled=True)
    piece = lax.all_gather(received, "dp", axis=0, tiled=True)
    result = expert_rows(piece.reshape(-1, width), gate_w, up_w, down_w)
    partials = result.reshape(piece.shape[0], piece.shape[1], width)
    summed = lax.psum_scatter(partials, "dp", scatter_dimension=0, tiled=True)
    back = lax.all_to_all(summed, "expert", split_axis=0, concat_axis=0, tiled=True)
    mixed = jnp.dot(mixing, back.reshape(-1, width), precision=lax.Precision.HIGHEST)
    return mixed.astype(jnp.bfloat16)


def tiles_of(total, step):
    return total // step, total % step


def kernel(experts, cap, tokens, ids, comb, gate_hbm, up_hbm, down_hbm, out,
           tok, contrib, from_core, from_b, from_a, from_z, picked, hid, gate_w, up_w, down_w,
           w_sem, send_sem, recv_sem, pair_send, pair_recv, ret_send, b_recv, a_recv, z_recv):
    rows, width = tokens.shape
    half = gate_w.shape[1]
    padded = tok.shape[2]
    top = ids.shape[1]
    groups = experts // 4
    span = 2 * groups
    me, dp = lax.axis_index("expert"), lax.axis_index("dp")
    core, side, g = me % 2, (me // 2) % 2, me // 4
    partner = (me + 1 - 2 * core, dp)
    a_peer = (me + (1 - core) * (2 - 4 * side), dp + core * (1 - 2 * dp))
    b_peer = (me + core * (2 - 4 * side), dp + (1 - core) * (1 - 2 * dp))

    def z_peer(j):
        return (((g + j) % groups) * 4 + me % 4, dp)

    loads = [
        pltpu.make_async_copy(gate_hbm.at[0], gate_w, w_sem.at[0]),
        pltpu.make_async_copy(up_hbm.at[0], up_w, w_sem.at[1]),
        pltpu.make_async_copy(down_hbm.at[0], down_w, w_sem.at[2]),
    ]

    edge = padded - 128
    own = width - edge
    lane = lax.broadcasted_iota(jnp.int32, (rows, 128), 1)
    hits = jnp.zeros((rows, 128), F32)
    weights = jnp.zeros((rows, 128), F32)
    for k in range(top):
        hits += jnp.where(lane == ids[:, k:k + 1] + own, 1.0, 0.0)
        weights += jnp.where(lane == ids[:, k:k + 1] + (own + experts), comb[:, k:k + 1].astype(F32), 0.0)
    below = (lax.broadcasted_iota(jnp.int32, (rows, rows), 0)
             >= lax.broadcasted_iota(jnp.int32, (rows, rows), 1)).astype(BF16)
    counts = jnp.dot(below, hits.astype(BF16), preferred_element_type=F32)
    info = (hits * counts + weights).astype(BF16)
    tok[0, :, :edge] = tokens[:, :edge]
    tok[0, :, edge:] = jnp.concatenate([tokens[:, edge:width], info[:, own:]], axis=1)

    barrier = pltpu.get_barrier_semaphore()
    peers = [partner, a_peer, b_peer] + [z_peer(j) for j in range(1, groups)]
    for peer in peers:
        pl.semaphore_signal(barrier, inc=1, device_id=peer, device_id_type=MESH)
    pl.semaphore_wait(barrier, len(peers))

    def place(k):
        return (k // groups) * span + k % groups

    def sent(src, dst, sem, peer):
        return pltpu.make_async_remote_copy(
            src_ref=tok.at[src], dst_ref=tok.at[dst], send_sem=send_sem.at[sem],
            recv_sem=recv_sem.at[dst], device_id=peer, device_id_type=MESH)

    def to_z(j):
        return sent(0, groups - j, j, z_peer(j))

    def to_a(j):
        return sent(place(j), place(groups + j), groups + j, a_peer)

    def to_b(k):
        return sent(place(k), place(2 * groups + k), 2 * groups + k, b_peer)

    def to_core(k):
        return sent(place(k), place(k) + groups, 4 * groups + k, partner)

    def arrived(slot):
        sent(0, slot, 0, partner).wait_recv()

    for j in range(1, groups):
        to_z(j).start()
    to_a(0).start()
    to_b(0).start()
    to_core(0).start()
    for load in loads:
        load.start()
    for j in range(1, groups):
        arrived(place(j))
        to_a(j).start()
        to_b(j).start()
        to_core(j).start()
    for j in range(groups):
        arrived(place(groups + j))
        to_b(groups + j).start()
        to_core(groups + j).start()
    for load in loads:
        load.wait()

    def pair_copy(c):
        return pltpu.make_async_remote_copy(
            src_ref=contrib.at[pl.ds(c * span + groups, groups)], dst_ref=from_core.at[pl.ds(c * groups, groups)],
            send_sem=pair_send.at[c], recv_sem=pair_recv.at[c], device_id=partner, device_id_type=MESH)

    def b_copy(k):
        return pltpu.make_async_remote_copy(
            src_ref=contrib.at[place(2 * groups + k)], dst_ref=from_b.at[k],
            send_sem=ret_send.at[2 * groups + k], recv_sem=b_recv.at[k], device_id=b_peer, device_id_type=MESH)

    def a_copy(j):
        return pltpu.make_async_remote_copy(
            src_ref=contrib.at[place(groups + j)], dst_ref=from_a.at[j],
            send_sem=ret_send.at[groups + j], recv_sem=a_recv.at[j], device_id=a_peer, device_id_type=MESH)

    def z_copy(j):
        return pltpu.make_async_remote_copy(
            src_ref=contrib.at[j], dst_ref=from_z.at[groups - j],
            send_sem=ret_send.at[j], recv_sem=z_recv.at[groups - j], device_id=z_peer(j), device_id_type=MESH)

    def back_to_b(c):
        pair_copy(c).wait_recv()

        def one(q, _):
            k = c * groups + q
            s = place(k)
            contrib[s] = (contrib[s].astype(F32) + from_core[k].astype(F32)).astype(BF16)
            b_copy(k - 2 * groups).start()
            return 0

        lax.fori_loop(0, groups, one, 0)

    chunk_rows = span * cap
    chunk_toks = span * rows

    def chunk(c):
        block = tok.at[pl.ds(c * span, span)]
        tail = block[:, :, edge:].reshape(chunk_toks, 128).astype(F32)
        tail_lane = lax.broadcasted_iota(jnp.int32, (chunk_toks, 128), 1)
        rank1 = jnp.sum(jnp.where(tail_lane == me + own, tail, 0.0), axis=1, keepdims=True)
        slot = (lax.broadcasted_iota(jnp.int32, (chunk_toks, 1), 0) // rows * cap).astype(F32)
        where_to = jnp.where(rank1 > 0.5, slot + rank1 - 1.0, -1.0)
        column = lax.broadcasted_iota(jnp.int32, (chunk_toks, chunk_rows), 1).astype(F32)
        select = (where_to == column).astype(BF16)
        step = 512
        select_t = select.T
        for n in range(0, padded, step):
            size = min(step, padded - n)
            part = block[:, :, n:n + size].reshape(chunk_toks, size)
            picked[:, n:n + size] = jnp.dot(select_t, part, preferred_element_type=F32).astype(BF16)
        row_tail = picked[:, edge:].astype(F32)
        row_lane = lax.broadcasted_iota(jnp.int32, (chunk_rows, 128), 1)
        scale = jnp.sum(jnp.where(row_lane == me + (own + experts), row_tail, 0.0), axis=1, keepdims=True) * (1.0 / 32.0)

        def ffn(cols):
            x = picked[:, :width]
            gate = jnp.dot(x, gate_w[:, cols], preferred_element_type=F32)
            up = jnp.dot(x, up_w[:, cols], preferred_element_type=F32)
            hid[:, cols] = (gate * jax.nn.sigmoid(1.702 * gate) * (up + 1.0)).astype(BF16)

        whole, rest = tiles_of(half, 256)

        def ffn_step(n, _):
            ffn(pl.ds(pl.multiple_of(n * 256, 256), 256))
            return 0

        lax.fori_loop(0, whole, ffn_step, 0)
        if rest:
            ffn(pl.ds(whole * 256, rest))

        def down(cols, size):
            res = jnp.dot(hid[...], down_w[:, cols], preferred_element_type=F32) * scale
            spread = jnp.dot(select, res.astype(BF16), preferred_element_type=F32).astype(BF16)
            contrib[pl.ds(c * span, span), :, cols] = spread.reshape(span, rows, size)

        whole2, rest2 = tiles_of(width, 512)

        def down_step(n, _):
            down(pl.ds(pl.multiple_of(n * 512, 512), 512), 512)
            return 0

        lax.fori_loop(0, whole2, down_step, 0)
        if rest2:
            down(pl.ds(whole2 * 512, rest2), rest2)

    def stage(i, _):
        c = 2 * i - i // 2 - 4 * (i // 3)

        @pl.when((i == 1) | (i == 2))
        def _():
            def one(q, _):
                k = c * groups + q
                arrived(place(k))
                to_core(k).start()
                return 0

            lax.fori_loop(0, groups, one, 0)

        def got(q, _):
            arrived(c * span + groups + q)
            return 0

        lax.fori_loop(0, groups, got, 0)

        @pl.when(i == 3)
        def _():
            back_to_b(3)

        chunk(c)
        pair_copy(c).start()

        @pl.when(i == 2)
        def _():
            back_to_b(2)

        return 0

    lax.fori_loop(0, 4, stage, 0)

    pair_copy(1).wait_recv()

    def a_step(j, _):
        b_copy(groups + j).wait_recv()
        s = place(groups + j)
        contrib[s] = (contrib[s].astype(F32) + from_core[groups + j].astype(F32)
                      + from_b[groups + j].astype(F32)).astype(BF16)
        a_copy(j).start()
        return 0

    lax.fori_loop(0, groups, a_step, 0)
    pair_copy(0).wait_recv()

    for j in list(range(1, groups)) + [0]:
        b_copy(j).wait_recv()
        a_copy(j).wait_recv()
        total = (contrib[j].astype(F32) + from_core[j].astype(F32)
                 + from_b[j].astype(F32) + from_a[j].astype(F32))
        if j:
            contrib[j] = total.astype(BF16)
            z_copy(j).start()
        else:
            for q in range(1, groups):
                z_copy(groups - q).wait_recv()
            for q in range(1, groups):
                total = total + from_z[q].astype(F32)
            out[...] = total.astype(BF16)

    for j in range(1, groups):
        to_z(j).wait_send()
        z_copy(j).wait_send()
    for j in range(groups):
        to_a(j).wait_send()
        a_copy(j).wait_send()
    for c in range(4):
        pair_copy(c).wait_send()
    for k in range(2 * groups):
        to_b(k).wait_send()
        b_copy(k).wait_send()
    for k in range(4 * groups):
        to_core(k).wait_send()


def gathered_plan(tokens, expert_ids, combine_int, gate_weight, up_weight, down_weight):
    experts = lax.axis_size("expert")
    rows, width = tokens.shape
    cap = 2 * expert_ids.shape[1] * rows // experts
    half = gate_weight.shape[2]
    groups = experts // 4
    padded = -(-width // 128) * 128
    span = 2 * groups
    vmem = pl.BlockSpec(memory_space=pltpu.VMEM)
    anywhere = pl.BlockSpec(memory_space=pl.ANY)
    dma = pltpu.SemaphoreType.DMA
    flops = 2 * 4 * span * cap * width * half * 3
    return pl.pallas_call(
        functools.partial(kernel, experts, cap),
        out_shape=jax.ShapeDtypeStruct((rows, width), BF16),
        in_specs=[vmem] * 3 + [anywhere] * 3,
        out_specs=vmem,
        scratch_shapes=[
            pltpu.VMEM((8 * groups, rows, padded), BF16),
            pltpu.VMEM((8 * groups, rows, width), BF16),
            pltpu.VMEM((4 * groups, rows, width), BF16),
            pltpu.VMEM((2 * groups, rows, width), BF16),
            pltpu.VMEM((groups, rows, width), BF16),
            pltpu.VMEM((groups, rows, width), BF16),
            pltpu.VMEM((span * cap, padded), BF16),
            pltpu.VMEM((span * cap, half), BF16),
            pltpu.VMEM((width, half), BF16),
            pltpu.VMEM((width, half), BF16),
            pltpu.VMEM((half, width), BF16),
            dma((3,)),
            dma((8 * groups,)),
            dma((8 * groups,)),
            dma((4,)),
            dma((4,)),
            dma((4 * groups,)),
            dma((2 * groups,)),
            dma((groups,)),
            dma((groups,)),
        ],
        compiler_params=pltpu.CompilerParams(
            collective_id=0, has_side_effects=True, vmem_limit_bytes=67043328),
        cost_estimate=pl.CostEstimate(flops=flops, bytes_accessed=6 * width * half, transcendentals=0),
    )(tokens, expert_ids, combine_int, gate_weight, up_weight, down_weight)


def shards(tokens, expert_ids, *rest):
    experts = lax.axis_size("expert")
    rows, width = tokens.shape
    cap = 2 * expert_ids.shape[1] * rows // experts
    gathers = 2 * cap >= rows and experts % 4 == 0 and width % 128 + 2 * experts <= 128 and rows % 16 == 0 and width % 128 > 0
    plan = gathered_plan if gathers else padded_plan
    return plan(tokens, expert_ids, *rest)


def solution(mesh):
    return jax.shard_map(
        shards,
        mesh=mesh,
        in_specs=(
            P(("expert", "dp"), None),
            P(("expert", "dp"), None),
            P(("expert", "dp"), None),
            P("expert", None, "dp"),
            P("expert", None, "dp"),
            P("expert", "dp", None),
        ),
        out_specs=P(("expert", "dp"), None),
        check_vma=False,
    )
```

```python
import functools

import jax
import jax.numpy as jnp
from jax import lax
from jax.experimental import pallas as pl
from jax.experimental.pallas import tpu as pltpu
from jax.sharding import PartitionSpec as P

MESH = pl.DeviceIdType.MESH
BF16 = jnp.bfloat16
F32 = jnp.float32
LAST = (((1,), (1,)), ((), ()))


def expert_rows(rows, gate_w, up_w, down_w):
    gate = jnp.dot(rows, gate_w, preferred_element_type=jnp.float32)
    up = jnp.dot(rows, up_w, preferred_element_type=jnp.float32)
    hidden = (gate * jax.nn.sigmoid(1.702 * gate) * (up + 1.0)).astype(jnp.bfloat16)
    return jnp.dot(hidden, down_w, preferred_element_type=jnp.float32)


def build_tables(tokens, expert_ids, combine_int, experts, capacity):
    tok_rows, top = expert_ids.shape
    flat_ids = expert_ids.reshape(-1)
    onehot = (flat_ids[:, None] == jnp.arange(experts, dtype=jnp.int32)[None, :]).astype(jnp.int32)
    ranks = jnp.sum(onehot * (jnp.cumsum(onehot, axis=0) - 1), axis=1)
    places = (flat_ids * capacity + ranks).reshape(tok_rows, top)
    slot_ids = jnp.arange(experts * capacity, dtype=jnp.int32)
    matches = places[:, :, None] == slot_ids[None, None, :]
    sender = jnp.any(matches, axis=1).astype(jnp.bfloat16)
    buffer = jnp.dot(sender.T, tokens, preferred_element_type=jnp.float32).astype(jnp.bfloat16)
    weights = combine_int.astype(jnp.float32) / 32.0
    mixing = jnp.sum(jnp.where(matches, weights[:, :, None], 0.0), axis=1)
    return (buffer.reshape(experts, capacity, tokens.shape[1]), mixing)


def padded_plan(tokens, expert_ids, combine_int, gate_weight, up_weight, down_weight):
    experts = lax.axis_size("expert")
    width = tokens.shape[1]
    capacity = 2 * expert_ids.shape[1] * tokens.shape[0] // experts
    gate_w, up_w, down_w = (gate_weight[0], up_weight[0], down_weight[0])
    buffer, mixing = build_tables(tokens, expert_ids, combine_int, experts, capacity)
    received = lax.all_to_all(buffer, "expert", split_axis=0, concat_axis=0, tiled=True)
    piece = lax.all_gather(received, "dp", axis=0, tiled=True)
    result = expert_rows(piece.reshape(-1, width), gate_w, up_w, down_w)
    partials = result.reshape(piece.shape[0], piece.shape[1], width)
    summed = lax.psum_scatter(partials, "dp", scatter_dimension=0, tiled=True)
    back = lax.all_to_all(summed, "expert", split_axis=0, concat_axis=0, tiled=True)
    mixed = jnp.dot(mixing, back.reshape(-1, width), precision=lax.Precision.HIGHEST)
    return mixed.astype(jnp.bfloat16)


def tiles_of(total, step):
    return total // step, total % step


def kernel(experts, cap, tokens, ids_t, comb_t, gate_hbm, up_hbm, down_hbm, out,
           tok, contrib, from_core, from_b, from_a, from_z, acc, picked, hid, gate_w, up_w, down_w,
           w_sem, send_sem, recv_sem, pair_send, pair_recv, ret_send, b_recv, a_recv,
           z_send, zr_send, z_recv):
    rows, width = tokens.shape
    half = gate_w.shape[0]
    padded = tok.shape[2]
    top = ids_t.shape[0]
    ids, comb = ids_t[...].T, comb_t[...].T
    groups = experts // 4
    span = 2 * groups
    me, dp = lax.axis_index("expert"), lax.axis_index("dp")
    core, side, g = me % 2, (me // 2) % 2, me // 4
    partner = (me + 1 - 2 * core, dp)
    a_peer = (me + (1 - core) * (2 - 4 * side), dp + core * (1 - 2 * dp))
    b_peer = (me + core * (2 - 4 * side), dp + (1 - core) * (1 - 2 * dp))

    def z_peer(way):
        return (me + 4 * way, dp)

    def follows(way):
        return g < groups - 1 if way > 0 else g > 0

    def inside(z):
        return (z >= 0) & (z < groups)

    loads = [
        pltpu.make_async_copy(gate_hbm.at[0], gate_w, w_sem.at[0]),
        pltpu.make_async_copy(up_hbm.at[0], up_w, w_sem.at[1]),
        pltpu.make_async_copy(down_hbm.at[0], down_w, w_sem.at[2]),
    ]

    for load in loads:
        load.start()
    barrier = pltpu.get_barrier_semaphore()
    for peer in (partner, a_peer, b_peer):
        pl.semaphore_signal(barrier, inc=1, device_id=peer, device_id_type=MESH)
    for way in (1, -1):
        @pl.when(follows(way))
        def _():
            pl.semaphore_signal(barrier, inc=1, device_id=z_peer(way), device_id_type=MESH)

    edge = padded - 128
    own = width - edge
    lane = lax.broadcasted_iota(jnp.int32, (rows, 128), 1)
    hits = jnp.zeros((rows, 128), F32)
    weights = jnp.zeros((rows, 128), F32)
    for k in range(top):
        hits += jnp.where(lane == ids[:, k:k + 1] + own, 1.0, 0.0)
        weights += jnp.where(lane == ids[:, k:k + 1] + (own + experts), comb[:, k:k + 1].astype(F32), 0.0)
    below = (lax.broadcasted_iota(jnp.int32, (rows, rows), 0)
             >= lax.broadcasted_iota(jnp.int32, (rows, rows), 1)).astype(BF16)
    counts = jnp.dot(below, hits.astype(BF16), preferred_element_type=F32)
    info = (hits * counts + weights).astype(BF16)
    tok[g, :, :edge] = tokens[:, :edge]
    tok[g, :, edge:] = jnp.concatenate([tokens[:, edge:width], info[:, own:]], axis=1)

    neighbours = (g + groups - 1) // groups + (2 * groups - 2 - g) // groups
    pl.semaphore_wait(barrier, 3 + neighbours)

    def place(k):
        return (k // groups) * span + k % groups

    def sent(src, dst, sem, peer):
        return pltpu.make_async_remote_copy(
            src_ref=tok.at[src], dst_ref=tok.at[dst], send_sem=send_sem.at[sem],
            recv_sem=recv_sem.at[dst], device_id=peer, device_id_type=MESH)

    def to_z(src, way):
        return pltpu.make_async_remote_copy(
            src_ref=tok.at[src], dst_ref=tok.at[src], send_sem=z_send.at[(1 - way) // 2, src],
            recv_sem=recv_sem.at[src], device_id=z_peer(way), device_id_type=MESH)

    def to_a(j):
        return sent(place(j), place(groups + j), groups + j, a_peer)

    def to_b(k):
        return sent(place(k), place(2 * groups + k), 2 * groups + k, b_peer)

    def to_core(k):
        return sent(place(k), place(k) + groups, 4 * groups + k, partner)

    def arrived(slot):
        sent(0, slot, 0, partner).wait_recv()

    def spread_out(k):
        to_a(k).start()
        to_b(k).start()
        to_core(k).start()

    def pass_on(z):
        arrived(place(groups + z))
        to_b(groups + z).start()
        to_core(groups + z).start()

    for way in (1, -1):
        @pl.when(follows(way))
        def _():
            to_z(g, way).start()
    spread_out(g)
    for d in range(1, groups + 1):
        if d < groups:
            for way in (1, -1):
                src = g - way * d

                @pl.when(inside(src))
                def _():
                    arrived(src)

                    @pl.when(follows(way))
                    def _():
                        to_z(src, way).start()

                    spread_out(src)
        for way in (1, -1) if d > 1 else (1,):
            src = g - way * (d - 1)

            @pl.when(inside(src))
            def _():
                pass_on(src)
    for load in loads:
        load.wait()

    def pair_copy(c):
        return pltpu.make_async_remote_copy(
            src_ref=contrib.at[pl.ds(c * span + groups, groups)], dst_ref=from_core.at[pl.ds(c * groups, groups)],
            send_sem=pair_send.at[c], recv_sem=pair_recv.at[c], device_id=partner, device_id_type=MESH)

    def b_copy(k):
        return pltpu.make_async_remote_copy(
            src_ref=contrib.at[place(2 * groups + k)], dst_ref=from_b.at[k],
            send_sem=ret_send.at[2 * groups + k], recv_sem=b_recv.at[k], device_id=b_peer, device_id_type=MESH)

    def a_copy(j):
        return pltpu.make_async_remote_copy(
            src_ref=contrib.at[place(groups + j)], dst_ref=from_a.at[j],
            send_sem=ret_send.at[groups + j], recv_sem=a_recv.at[j], device_id=a_peer, device_id_type=MESH)

    def z_copy(z, way):
        return pltpu.make_async_remote_copy(
            src_ref=contrib.at[z], dst_ref=from_z.at[(1 - way) // 2, z],
            send_sem=zr_send.at[(1 - way) // 2, z], recv_sem=z_recv.at[(1 - way) // 2, z],
            device_id=z_peer(way), device_id_type=MESH)

    upper = g // (groups // 2)

    def far_first(t):
        return t * upper + (groups - 1 - t) * (1 - upper)

    def back_to_b(c):
        pair_copy(c).wait_recv()

        def one(q, _):
            k = c * groups + far_first(q)
            s = place(k)
            contrib[s] = (contrib[s].astype(F32) + from_core[k].astype(F32)).astype(BF16)
            b_copy(k - 2 * groups).start()
            return 0

        lax.fori_loop(0, groups, one, 0)

    chunk_rows = span * cap
    chunk_toks = span * rows

    def chunk(c):
        block = tok.at[pl.ds(c * span, span)]
        tail = block[:, :, edge:].reshape(chunk_toks, 128).astype(F32)
        tail_lane = lax.broadcasted_iota(jnp.int32, (chunk_toks, 128), 1)
        rank1 = jnp.sum(jnp.where(tail_lane == me + own, tail, 0.0), axis=1, keepdims=True)
        slot = (lax.broadcasted_iota(jnp.int32, (chunk_toks, 1), 0) // rows * cap).astype(F32)
        where_to = jnp.where(rank1 > 0.5, slot + rank1 - 1.0, -1.0)
        column = lax.broadcasted_iota(jnp.int32, (chunk_toks, chunk_rows), 1).astype(F32)
        select = (where_to == column).astype(BF16)
        step = 512
        select_t = select.T
        for n in range(0, padded, step):
            size = min(step, padded - n)
            part = block[:, :, n:n + size].reshape(chunk_toks, size)
            picked[:, n:n + size] = jnp.dot(select_t, part, preferred_element_type=F32).astype(BF16)
        row_tail = picked[:, edge:].astype(F32)
        row_lane = lax.broadcasted_iota(jnp.int32, (chunk_rows, 128), 1)
        scale = jnp.sum(jnp.where(row_lane == me + (own + experts), row_tail, 0.0), axis=1, keepdims=True) * (1.0 / 32.0)

        def ffn(cols):
            x = picked[:, :width]
            gate = lax.dot_general(x, gate_w[cols, :], LAST, preferred_element_type=F32)
            up = lax.dot_general(x, up_w[cols, :], LAST, preferred_element_type=F32)
            hid[:, cols] = (gate * jax.nn.sigmoid(1.702 * gate) * (up + 1.0)).astype(BF16)

        whole, rest = tiles_of(half, 256)

        def ffn_step(n, _):
            ffn(pl.ds(pl.multiple_of(n * 256, 256), 256))
            return 0

        lax.fori_loop(0, whole, ffn_step, 0)
        if rest:
            ffn(pl.ds(whole * 256, rest))

        def down(cols, size):
            res = jnp.dot(hid[...], down_w[:, cols], preferred_element_type=F32) * scale
            spread = jnp.dot(select, res.astype(BF16), preferred_element_type=F32).astype(BF16)
            contrib[pl.ds(c * span, span), :, cols] = spread.reshape(span, rows, size)

        whole2, rest2 = tiles_of(width, 512)

        def down_step(n, _):
            down(pl.ds(pl.multiple_of(n * 512, 512), 512), 512)
            return 0

        lax.fori_loop(0, whole2, down_step, 0)
        if rest2:
            down(pl.ds(whole2 * 512, rest2), rest2)

    def stage(i, _):
        c = (4 - i) % 4

        @pl.when(i == 1)
        def _():
            def one(q, _):
                k = 2 * groups + q
                arrived(place(k))
                to_core(k).start()
                return 0

            lax.fori_loop(0, 2 * groups, one, 0)

        def got(q, _):
            arrived(c * span + groups + q)
            return 0

        lax.fori_loop(0, groups, got, 0)

        @pl.when(i == 3)
        def _():
            back_to_b(2)

        chunk(c)
        pair_copy(c).start()

        @pl.when(i == 2)
        def _():
            back_to_b(3)

        return 0

    lax.fori_loop(0, 4, stage, 0)

    pair_copy(1).wait_recv()

    def a_step(t, _):
        j = far_first(t)
        b_copy(groups + j).wait_recv()
        s = place(groups + j)
        contrib[s] = (contrib[s].astype(F32) + from_core[groups + j].astype(F32)
                      + from_b[groups + j].astype(F32)).astype(BF16)
        a_copy(j).start()
        return 0

    lax.fori_loop(0, groups, a_step, 0)
    pair_copy(0).wait_recv()

    def gathered(z):
        return (contrib[z].astype(F32) + from_core[z].astype(F32)
                + from_b[z].astype(F32) + from_a[z].astype(F32))

    def z_step(t, _):
        z = far_first(t)
        b_copy(z).wait_recv()
        a_copy(z).wait_recv()
        acc[...] = gathered(z)
        for way in (1, -1):
            @pl.when((z - g) * way > 0)
            def _():
                @pl.when(follows(-way))
                def _():
                    z_copy(z, way).wait_recv()
                    acc[...] += from_z[(1 - way) // 2, z].astype(F32)

                contrib[z] = acc[...].astype(BF16)
                z_copy(z, way).start()

        return 0

    lax.fori_loop(0, groups, z_step, 0)
    acc[...] = gathered(g)
    for way in (1, -1):
        @pl.when(follows(-way))
        def _():
            z_copy(g, way).wait_recv()
            acc[...] += from_z[(1 - way) // 2, g].astype(F32)
    out[...] = acc[...].astype(BF16)

    for z in range(groups):
        for way in (1, -1):
            @pl.when(follows(way) & ((g - z) * way >= 0))
            def _():
                to_z(z, way).wait_send()

            @pl.when((z - g) * way > 0)
            def _():
                z_copy(z, way).wait_send()
        to_a(z).wait_send()
        a_copy(z).wait_send()
    for c in range(4):
        pair_copy(c).wait_send()
    for k in range(2 * groups):
        to_b(k).wait_send()
        b_copy(k).wait_send()
    for k in range(4 * groups):
        to_core(k).wait_send()


def gathered_plan(tokens, expert_ids, combine_int, gate_weight, up_weight, down_weight):
    experts = lax.axis_size("expert")
    rows, width = tokens.shape
    cap = 2 * expert_ids.shape[1] * rows // experts
    half = gate_weight.shape[2]
    groups = experts // 4
    padded = -(-width // 128) * 128
    span = 2 * groups
    vmem = pl.BlockSpec(memory_space=pltpu.VMEM)
    anywhere = pl.BlockSpec(memory_space=pl.ANY)
    dma = pltpu.SemaphoreType.DMA
    flops = 2 * 4 * span * cap * width * half * 3
    return pl.pallas_call(
        functools.partial(kernel, experts, cap),
        out_shape=jax.ShapeDtypeStruct((rows, width), BF16),
        in_specs=[vmem] * 3 + [anywhere] * 3,
        out_specs=vmem,
        scratch_shapes=[
            pltpu.VMEM((8 * groups, rows, padded), BF16),
            pltpu.VMEM((8 * groups, rows, width), BF16),
            pltpu.VMEM((4 * groups, rows, width), BF16),
            pltpu.VMEM((2 * groups, rows, width), BF16),
            pltpu.VMEM((groups, rows, width), BF16),
            pltpu.VMEM((2, groups, rows, width), BF16),
            pltpu.VMEM((rows, width), F32),
            pltpu.VMEM((span * cap, padded), BF16),
            pltpu.VMEM((span * cap, half), BF16),
            pltpu.VMEM((half, width), BF16),
            pltpu.VMEM((half, width), BF16),
            pltpu.VMEM((half, width), BF16),
            dma((3,)),
            dma((8 * groups,)),
            dma((8 * groups,)),
            dma((4,)),
            dma((4,)),
            dma((4 * groups,)),
            dma((2 * groups,)),
            dma((groups,)),
            dma((2, groups)),
            dma((2, groups)),
            dma((2, groups)),
        ],
        compiler_params=pltpu.CompilerParams(
            collective_id=0, has_side_effects=True, vmem_limit_bytes=67043328),
        cost_estimate=pl.CostEstimate(flops=flops, bytes_accessed=6 * width * half, transcendentals=0),
    )(tokens, expert_ids.T, combine_int.T, jnp.swapaxes(gate_weight, 1, 2), jnp.swapaxes(up_weight, 1, 2), down_weight)


def shards(tokens, expert_ids, *rest):
    experts = lax.axis_size("expert")
    rows, width = tokens.shape
    cap = 2 * expert_ids.shape[1] * rows // experts
    gathers = 2 * cap >= rows and experts % 4 == 0 and width % 128 + 2 * experts <= 128 and rows % 16 == 0 and width % 128 > 0
    plan = gathered_plan if gathers else padded_plan
    return plan(tokens, expert_ids, *rest)


def solution(mesh):
    return jax.shard_map(
        shards,
        mesh=mesh,
        in_specs=(
            P(("expert", "dp"), None),
            P(("expert", "dp"), None),
            P(("expert", "dp"), None),
            P("expert", None, "dp"),
            P("expert", None, "dp"),
            P("expert", "dp", None),
        ),
        out_specs=P(("expert", "dp"), None),
        check_vma=False,
    )
```

```python
import functools

import jax
import jax.numpy as jnp
from jax import lax
from jax.experimental import pallas as pl
from jax.experimental.pallas import tpu as pltpu
from jax.sharding import PartitionSpec as P

MESH = pl.DeviceIdType.MESH
BF16 = jnp.bfloat16
F32 = jnp.float32
LAST = (((1,), (1,)), ((), ()))
PAUSE = 0
FTILE = 768
DTILE = 1408


def expert_rows(rows, gate_w, up_w, down_w):
    gate = jnp.dot(rows, gate_w, preferred_element_type=jnp.float32)
    up = jnp.dot(rows, up_w, preferred_element_type=jnp.float32)
    hidden = (gate * jax.nn.sigmoid(1.702 * gate) * (up + 1.0)).astype(jnp.bfloat16)
    return jnp.dot(hidden, down_w, preferred_element_type=jnp.float32)


def build_tables(tokens, expert_ids, combine_int, experts, capacity):
    tok_rows, top = expert_ids.shape
    flat_ids = expert_ids.reshape(-1)
    onehot = (flat_ids[:, None] == jnp.arange(experts, dtype=jnp.int32)[None, :]).astype(jnp.int32)
    ranks = jnp.sum(onehot * (jnp.cumsum(onehot, axis=0) - 1), axis=1)
    places = (flat_ids * capacity + ranks).reshape(tok_rows, top)
    slot_ids = jnp.arange(experts * capacity, dtype=jnp.int32)
    matches = places[:, :, None] == slot_ids[None, None, :]
    sender = jnp.any(matches, axis=1).astype(jnp.bfloat16)
    buffer = jnp.dot(sender.T, tokens, preferred_element_type=jnp.float32).astype(jnp.bfloat16)
    weights = combine_int.astype(jnp.float32) / 32.0
    mixing = jnp.sum(jnp.where(matches, weights[:, :, None], 0.0), axis=1)
    return (buffer.reshape(experts, capacity, tokens.shape[1]), mixing)


def padded_plan(tokens, expert_ids, combine_int, gate_weight, up_weight, down_weight):
    experts = lax.axis_size("expert")
    width = tokens.shape[1]
    capacity = 2 * expert_ids.shape[1] * tokens.shape[0] // experts
    gate_w, up_w, down_w = (gate_weight[0], up_weight[0], down_weight[0])
    buffer, mixing = build_tables(tokens, expert_ids, combine_int, experts, capacity)
    received = lax.all_to_all(buffer, "expert", split_axis=0, concat_axis=0, tiled=True)
    piece = lax.all_gather(received, "dp", axis=0, tiled=True)
    result = expert_rows(piece.reshape(-1, width), gate_w, up_w, down_w)
    partials = result.reshape(piece.shape[0], piece.shape[1], width)
    summed = lax.psum_scatter(partials, "dp", scatter_dimension=0, tiled=True)
    back = lax.all_to_all(summed, "expert", split_axis=0, concat_axis=0, tiled=True)
    mixed = jnp.dot(mixing, back.reshape(-1, width), precision=lax.Precision.HIGHEST)
    return mixed.astype(jnp.bfloat16)


def tiles_of(total, step):
    return total // step, total % step


def kernel(experts, cap, tokens, ids_t, comb_t, gate_hbm, up_hbm, down_hbm, out,
           tok, contrib, from_core, from_b, from_a, from_z, acc, picked, hid, gate_w, up_w, down_w,
           w_sem, send_sem, recv_sem, pair_send, pair_recv, ret_send, b_recv, a_recv,
           z_send, zr_send, z_recv):
    rows, width = tokens.shape
    half = gate_w.shape[0]
    padded = tok.shape[2]
    top = ids_t.shape[0]
    ids, comb = ids_t[...].T, comb_t[...].T
    groups = experts // 4
    span = 2 * groups
    me, dp = lax.axis_index("expert"), lax.axis_index("dp")
    core, side, g = me % 2, (me // 2) % 2, me // 4
    partner = (me + 1 - 2 * core, dp)
    a_peer = (me + (1 - core) * (2 - 4 * side), dp + core * (1 - 2 * dp))
    b_peer = (me + core * (2 - 4 * side), dp + (1 - core) * (1 - 2 * dp))

    def z_peer(way):
        return (me + 4 * way, dp)

    def follows(way):
        return g < groups - 1 if way > 0 else g > 0

    def inside(z):
        return (z >= 0) & (z < groups)

    loads = [
        pltpu.make_async_copy(gate_hbm.at[0], gate_w, w_sem.at[0]),
        pltpu.make_async_copy(up_hbm.at[0], up_w, w_sem.at[1]),
        pltpu.make_async_copy(down_hbm.at[0], down_w, w_sem.at[2]),
    ]

    for load in loads:
        load.start()
    barrier = pltpu.get_barrier_semaphore()
    for peer in (partner, a_peer, b_peer):
        pl.semaphore_signal(barrier, inc=1, device_id=peer, device_id_type=MESH)
    for way in (1, -1):
        @pl.when(follows(way))
        def _():
            pl.semaphore_signal(barrier, inc=1, device_id=z_peer(way), device_id_type=MESH)

    edge = padded - 128
    own = width - edge
    lane = lax.broadcasted_iota(jnp.int32, (rows, 128), 1)
    hits = jnp.zeros((rows, 128), F32)
    weights = jnp.zeros((rows, 128), F32)
    for k in range(top):
        hits += jnp.where(lane == ids[:, k:k + 1] + own, 1.0, 0.0)
        weights += jnp.where(lane == ids[:, k:k + 1] + (own + experts), comb[:, k:k + 1].astype(F32), 0.0)
    below = (lax.broadcasted_iota(jnp.int32, (rows, rows), 0)
             >= lax.broadcasted_iota(jnp.int32, (rows, rows), 1)).astype(BF16)
    counts = jnp.dot(below, hits.astype(BF16), preferred_element_type=F32)
    info = (hits * counts + weights).astype(BF16)
    tok[g, :, :edge] = tokens[:, :edge]
    tok[g, :, edge:] = jnp.concatenate([tokens[:, edge:width], info[:, own:]], axis=1)

    neighbours = (g + groups - 1) // groups + (2 * groups - 2 - g) // groups
    pl.semaphore_wait(barrier, 3 + neighbours)

    def place(k):
        return (k // groups) * span + k % groups

    def sent(src, dst, sem, peer):
        return pltpu.make_async_remote_copy(
            src_ref=tok.at[src], dst_ref=tok.at[dst], send_sem=send_sem.at[sem],
            recv_sem=recv_sem.at[dst], device_id=peer, device_id_type=MESH)

    def to_z(src, way):
        return pltpu.make_async_remote_copy(
            src_ref=tok.at[src], dst_ref=tok.at[src], send_sem=z_send.at[(1 - way) // 2, src],
            recv_sem=recv_sem.at[src], device_id=z_peer(way), device_id_type=MESH)

    def to_a(j):
        return sent(place(j), place(groups + j), groups + j, a_peer)

    def to_b(k):
        return sent(place(k), place(2 * groups + k), 2 * groups + k, b_peer)

    def to_core(k):
        return sent(place(k), place(k) + groups, 4 * groups + k, partner)

    def arrived(slot):
        sent(0, slot, 0, partner).wait_recv()

    def spread_out(k):
        to_a(k).start()
        to_b(k).start()
        to_core(k).start()

    def pass_on(z):
        arrived(place(groups + z))
        to_b(groups + z).start()
        to_core(groups + z).start()

    for way in (1, -1):
        @pl.when(follows(way))
        def _():
            to_z(g, way).start()
    spread_out(g)
    for d in range(1, groups + 1):
        if d < groups:
            for way in (1, -1):
                src = g - way * d

                @pl.when(inside(src))
                def _():
                    arrived(src)

                    @pl.when(follows(way))
                    def _():
                        to_z(src, way).start()

                    spread_out(src)
        for way in (1, -1) if d > 1 else (1,):
            src = g - way * (d - 1)

            @pl.when(inside(src))
            def _():
                pass_on(src)
    for load in loads:
        load.wait()

    def pair_copy(c):
        return pltpu.make_async_remote_copy(
            src_ref=contrib.at[pl.ds(c * span + groups, groups)], dst_ref=from_core.at[pl.ds(c * groups, groups)],
            send_sem=pair_send.at[c], recv_sem=pair_recv.at[c], device_id=partner, device_id_type=MESH)

    def b_copy(k):
        return pltpu.make_async_remote_copy(
            src_ref=contrib.at[place(2 * groups + k)], dst_ref=from_b.at[k],
            send_sem=ret_send.at[2 * groups + k], recv_sem=b_recv.at[k], device_id=b_peer, device_id_type=MESH)

    def a_copy(j):
        return pltpu.make_async_remote_copy(
            src_ref=contrib.at[place(groups + j)], dst_ref=from_a.at[j],
            send_sem=ret_send.at[groups + j], recv_sem=a_recv.at[j], device_id=a_peer, device_id_type=MESH)

    def z_copy(z, way):
        return pltpu.make_async_remote_copy(
            src_ref=contrib.at[z], dst_ref=from_z.at[(1 - way) // 2, z],
            send_sem=zr_send.at[(1 - way) // 2, z], recv_sem=z_recv.at[(1 - way) // 2, z],
            device_id=z_peer(way), device_id_type=MESH)

    upper = g // (groups // 2)

    def far_first(t):
        return t * upper + (groups - 1 - t) * (1 - upper)

    def back_to_b(c):
        pair_copy(c).wait_recv()

        def one(q, _):
            k = c * groups + far_first(q)
            s = place(k)
            contrib[s] = (contrib[s].astype(F32) + from_core[k].astype(F32)).astype(BF16)
            b_copy(k - 2 * groups).start()
            return 0

        lax.fori_loop(0, groups, one, 0)

    chunk_rows = span * cap
    chunk_toks = span * rows

    def chunk(c, meanwhile):
        block = tok.at[pl.ds(c * span, span)]
        tail = block[:, :, edge:].reshape(chunk_toks, 128).astype(F32)
        tail_lane = lax.broadcasted_iota(jnp.int32, (chunk_toks, 128), 1)
        rank1 = jnp.sum(jnp.where(tail_lane == me + own, tail, 0.0), axis=1, keepdims=True)
        slot = (lax.broadcasted_iota(jnp.int32, (chunk_toks, 1), 0) // rows * cap).astype(F32)
        where_to = jnp.where(rank1 > 0.5, slot + rank1 - 1.0, -1.0)
        column = lax.broadcasted_iota(jnp.int32, (chunk_toks, chunk_rows), 1).astype(F32)
        select = (where_to == column).astype(BF16)
        step = 512
        select_t = select.T
        for n in range(0, padded, step):
            size = min(step, padded - n)
            part = block[:, :, n:n + size].reshape(chunk_toks, size)
            picked[:, n:n + size] = jnp.dot(select_t, part, preferred_element_type=F32).astype(BF16)
        row_tail = picked[:, edge:].astype(F32)
        row_lane = lax.broadcasted_iota(jnp.int32, (chunk_rows, 128), 1)
        scale = jnp.sum(jnp.where(row_lane == me + (own + experts), row_tail, 0.0), axis=1, keepdims=True) * (1.0 / 32.0)

        def ffn(cols):
            x = picked[:, :width]
            gate = lax.dot_general(x, gate_w[cols, :], LAST, preferred_element_type=F32)
            up = lax.dot_general(x, up_w[cols, :], LAST, preferred_element_type=F32)
            hid[:, cols] = (gate * jax.nn.sigmoid(1.702 * gate) * (up + 1.0)).astype(BF16)

        whole, rest = tiles_of(half, FTILE)

        def ffn_step(n, _):
            meanwhile(n)
            ffn(pl.ds(pl.multiple_of(n * FTILE, FTILE), FTILE))
            return 0

        lax.fori_loop(0, whole, ffn_step, 0)
        if rest:
            ffn(pl.ds(whole * FTILE, rest))

        def down(cols, size):
            res = jnp.dot(hid[...], down_w[:, cols], preferred_element_type=F32) * scale
            spread = jnp.dot(select, res.astype(BF16), preferred_element_type=F32).astype(BF16)
            contrib[pl.ds(c * span, span), :, cols] = spread.reshape(span, rows, size)

        whole2, rest2 = tiles_of(width, DTILE)

        def down_step(n, _):
            down(pl.ds(pl.multiple_of(n * DTILE, DTILE), DTILE), DTILE)
            return 0

        lax.fori_loop(0, whole2, down_step, 0)
        if rest2:
            down(pl.ds(whole2 * DTILE, rest2), rest2)

    def stage(i, _):
        c = (4 - i) % 4

        @pl.when(i == 1)
        def _():
            def one(q, _):
                k = 2 * groups + q
                arrived(place(k))
                to_core(k).start()
                return 0

            lax.fori_loop(0, 2 * groups, one, 0)

        def got(q, _):
            arrived(c * span + groups + q)
            return 0

        lax.fori_loop(0, groups, got, 0)

        def meanwhile(n):
            @pl.when((n == PAUSE) & (i >= 2))
            def _():
                back_to_b((c + 1) % 4)

        chunk(c, meanwhile)
        pair_copy(c).start()
        return 0

    lax.fori_loop(0, 4, stage, 0)

    pair_copy(1).wait_recv()

    def a_step(t, _):
        j = far_first(t)
        b_copy(groups + j).wait_recv()
        s = place(groups + j)
        contrib[s] = (contrib[s].astype(F32) + from_core[groups + j].astype(F32)
                      + from_b[groups + j].astype(F32)).astype(BF16)
        a_copy(j).start()
        return 0

    lax.fori_loop(0, groups, a_step, 0)
    pair_copy(0).wait_recv()

    def gathered(z):
        return (contrib[z].astype(F32) + from_core[z].astype(F32)
                + from_b[z].astype(F32) + from_a[z].astype(F32))

    def z_step(t, _):
        z = far_first(t)
        b_copy(z).wait_recv()
        a_copy(z).wait_recv()
        acc[...] = gathered(z)
        for way in (1, -1):
            @pl.when((z - g) * way > 0)
            def _():
                @pl.when(follows(-way))
                def _():
                    z_copy(z, way).wait_recv()
                    acc[...] += from_z[(1 - way) // 2, z].astype(F32)

                contrib[z] = acc[...].astype(BF16)
                z_copy(z, way).start()

        return 0

    lax.fori_loop(0, groups, z_step, 0)
    acc[...] = gathered(g)
    for way in (1, -1):
        @pl.when(follows(-way))
        def _():
            z_copy(g, way).wait_recv()
            acc[...] += from_z[(1 - way) // 2, g].astype(F32)
    out[...] = acc[...].astype(BF16)

    for z in range(groups):
        for way in (1, -1):
            @pl.when(follows(way) & ((g - z) * way >= 0))
            def _():
                to_z(z, way).wait_send()

            @pl.when((z - g) * way > 0)
            def _():
                z_copy(z, way).wait_send()
        to_a(z).wait_send()
        a_copy(z).wait_send()
    for c in range(4):
        pair_copy(c).wait_send()
    for k in range(2 * groups):
        to_b(k).wait_send()
        b_copy(k).wait_send()
    for k in range(4 * groups):
        to_core(k).wait_send()


def gathered_plan(tokens, expert_ids, combine_int, gate_weight, up_weight, down_weight):
    experts = lax.axis_size("expert")
    rows, width = tokens.shape
    cap = 2 * expert_ids.shape[1] * rows // experts
    half = gate_weight.shape[2]
    groups = experts // 4
    padded = -(-width // 128) * 128
    span = 2 * groups
    vmem = pl.BlockSpec(memory_space=pltpu.VMEM)
    anywhere = pl.BlockSpec(memory_space=pl.ANY)
    dma = pltpu.SemaphoreType.DMA
    flops = 2 * 4 * span * cap * width * half * 3
    return pl.pallas_call(
        functools.partial(kernel, experts, cap),
        out_shape=jax.ShapeDtypeStruct((rows, width), BF16),
        in_specs=[vmem] * 3 + [anywhere] * 3,
        out_specs=vmem,
        scratch_shapes=[
            pltpu.VMEM((8 * groups, rows, padded), BF16),
            pltpu.VMEM((8 * groups, rows, width), BF16),
            pltpu.VMEM((4 * groups, rows, width), BF16),
            pltpu.VMEM((2 * groups, rows, width), BF16),
            pltpu.VMEM((groups, rows, width), BF16),
            pltpu.VMEM((2, groups, rows, width), BF16),
            pltpu.VMEM((rows, width), F32),
            pltpu.VMEM((span * cap, padded), BF16),
            pltpu.VMEM((span * cap, half), BF16),
            pltpu.VMEM((half, width), BF16),
            pltpu.VMEM((half, width), BF16),
            pltpu.VMEM((half, width), BF16),
            dma((3,)),
            dma((8 * groups,)),
            dma((8 * groups,)),
            dma((4,)),
            dma((4,)),
            dma((4 * groups,)),
            dma((2 * groups,)),
            dma((groups,)),
            dma((2, groups)),
            dma((2, groups)),
            dma((2, groups)),
        ],
        compiler_params=pltpu.CompilerParams(
            collective_id=0, has_side_effects=True, vmem_limit_bytes=67043328),
        cost_estimate=pl.CostEstimate(flops=flops, bytes_accessed=6 * width * half, transcendentals=0),
    )(tokens, expert_ids.T, combine_int.T, jnp.swapaxes(gate_weight, 1, 2), jnp.swapaxes(up_weight, 1, 2), down_weight)


def shards(tokens, expert_ids, *rest):
    experts = lax.axis_size("expert")
    rows, width = tokens.shape
    cap = 2 * expert_ids.shape[1] * rows // experts
    gathers = 2 * cap >= rows and experts % 4 == 0 and width % 128 + 2 * experts <= 128 and rows % 16 == 0 and width % 128 > 0
    plan = gathered_plan if gathers else padded_plan
    return plan(tokens, expert_ids, *rest)


def solution(mesh):
    return jax.shard_map(
        shards,
        mesh=mesh,
        in_specs=(
            P(("expert", "dp"), None),
            P(("expert", "dp"), None),
            P(("expert", "dp"), None),
            P("expert", None, "dp"),
            P("expert", None, "dp"),
            P("expert", "dp", None),
        ),
        out_specs=P(("expert", "dp"), None),
        check_vma=False,
    )
```

```python
import functools

import jax
import jax.numpy as jnp
from jax import lax
from jax.experimental import pallas as pl
from jax.experimental.pallas import tpu as pltpu
from jax.sharding import PartitionSpec as P

MESH = pl.DeviceIdType.MESH
BF16 = jnp.bfloat16
F32 = jnp.float32
LAST = (((1,), (1,)), ((), ()))
PAUSE = 0
FTILE = 768
DTILE = 1536


def expert_rows(rows, gate_w, up_w, down_w):
    gate = jnp.dot(rows, gate_w, preferred_element_type=jnp.float32)
    up = jnp.dot(rows, up_w, preferred_element_type=jnp.float32)
    hidden = (gate * jax.nn.sigmoid(1.702 * gate) * (up + 1.0)).astype(jnp.bfloat16)
    return jnp.dot(hidden, down_w, preferred_element_type=jnp.float32)


def build_tables(tokens, expert_ids, combine_int, experts, capacity):
    tok_rows, top = expert_ids.shape
    flat_ids = expert_ids.reshape(-1)
    onehot = (flat_ids[:, None] == jnp.arange(experts, dtype=jnp.int32)[None, :]).astype(jnp.int32)
    ranks = jnp.sum(onehot * (jnp.cumsum(onehot, axis=0) - 1), axis=1)
    places = (flat_ids * capacity + ranks).reshape(tok_rows, top)
    slot_ids = jnp.arange(experts * capacity, dtype=jnp.int32)
    matches = places[:, :, None] == slot_ids[None, None, :]
    sender = jnp.any(matches, axis=1).astype(jnp.bfloat16)
    buffer = jnp.dot(sender.T, tokens, preferred_element_type=jnp.float32).astype(jnp.bfloat16)
    weights = combine_int.astype(jnp.float32) / 32.0
    mixing = jnp.sum(jnp.where(matches, weights[:, :, None], 0.0), axis=1)
    return (buffer.reshape(experts, capacity, tokens.shape[1]), mixing)


def padded_plan(tokens, expert_ids, combine_int, gate_weight, up_weight, down_weight):
    experts = lax.axis_size("expert")
    width = tokens.shape[1]
    capacity = 2 * expert_ids.shape[1] * tokens.shape[0] // experts
    gate_w, up_w, down_w = (gate_weight[0], up_weight[0], down_weight[0])
    buffer, mixing = build_tables(tokens, expert_ids, combine_int, experts, capacity)
    received = lax.all_to_all(buffer, "expert", split_axis=0, concat_axis=0, tiled=True)
    piece = lax.all_gather(received, "dp", axis=0, tiled=True)
    result = expert_rows(piece.reshape(-1, width), gate_w, up_w, down_w)
    partials = result.reshape(piece.shape[0], piece.shape[1], width)
    summed = lax.psum_scatter(partials, "dp", scatter_dimension=0, tiled=True)
    back = lax.all_to_all(summed, "expert", split_axis=0, concat_axis=0, tiled=True)
    mixed = jnp.dot(mixing, back.reshape(-1, width), precision=lax.Precision.HIGHEST)
    return mixed.astype(jnp.bfloat16)


def tiles_of(total, step):
    return total // step, total % step


def kernel(experts, cap, tokens, ids_t, comb_t, gate_hbm, up_hbm, down_hbm, out,
           tok, contrib, from_core, from_b, from_a, from_z, acc, picked, hid, gate_w, up_w, down_w,
           w_sem, send_sem, recv_sem, pair_send, pair_recv, ret_send, b_recv, a_recv,
           z_send, zr_send, z_recv):
    rows, width = tokens.shape
    half = gate_w.shape[0]
    padded = tok.shape[2]
    top = ids_t.shape[0]
    ids, comb = ids_t[...].T, comb_t[...].T
    groups = experts // 4
    span = 2 * groups
    me, dp = lax.axis_index("expert"), lax.axis_index("dp")
    core, side, g = me % 2, (me // 2) % 2, me // 4
    partner = (me + 1 - 2 * core, dp)
    a_peer = (me + (1 - core) * (2 - 4 * side), dp + core * (1 - 2 * dp))
    b_peer = (me + core * (2 - 4 * side), dp + (1 - core) * (1 - 2 * dp))

    def z_peer(way):
        return (me + 4 * way, dp)

    def follows(way):
        return g < groups - 1 if way > 0 else g > 0

    def inside(z):
        return (z >= 0) & (z < groups)

    loads = [
        pltpu.make_async_copy(gate_hbm.at[0], gate_w, w_sem.at[0]),
        pltpu.make_async_copy(up_hbm.at[0], up_w, w_sem.at[1]),
        pltpu.make_async_copy(down_hbm.at[0], down_w, w_sem.at[2]),
    ]

    for load in loads:
        load.start()
    barrier = pltpu.get_barrier_semaphore()
    for peer in (partner, a_peer, b_peer):
        pl.semaphore_signal(barrier, inc=1, device_id=peer, device_id_type=MESH)
    for way in (1, -1):
        @pl.when(follows(way))
        def _():
            pl.semaphore_signal(barrier, inc=1, device_id=z_peer(way), device_id_type=MESH)

    edge = padded - 128
    own = width - edge
    lane = lax.broadcasted_iota(jnp.int32, (rows, 128), 1)
    hits = jnp.zeros((rows, 128), F32)
    weights = jnp.zeros((rows, 128), F32)
    for k in range(top):
        hits += jnp.where(lane == ids[:, k:k + 1] + own, 1.0, 0.0)
        weights += jnp.where(lane == ids[:, k:k + 1] + (own + experts), comb[:, k:k + 1].astype(F32), 0.0)
    below = (lax.broadcasted_iota(jnp.int32, (rows, rows), 0)
             >= lax.broadcasted_iota(jnp.int32, (rows, rows), 1)).astype(BF16)
    counts = jnp.dot(below, hits.astype(BF16), preferred_element_type=F32)
    info = (hits * counts + weights).astype(BF16)
    tok[g, :, :edge] = tokens[:, :edge]
    tok[g, :, edge:] = jnp.concatenate([tokens[:, edge:width], info[:, own:]], axis=1)

    neighbours = (g + groups - 1) // groups + (2 * groups - 2 - g) // groups
    pl.semaphore_wait(barrier, 3 + neighbours)

    def place(k):
        return (k // groups) * span + k % groups

    def sent(src, dst, sem, peer):
        return pltpu.make_async_remote_copy(
            src_ref=tok.at[src], dst_ref=tok.at[dst], send_sem=send_sem.at[sem],
            recv_sem=recv_sem.at[dst], device_id=peer, device_id_type=MESH)

    def to_z(src, way):
        return pltpu.make_async_remote_copy(
            src_ref=tok.at[src], dst_ref=tok.at[src], send_sem=z_send.at[(1 - way) // 2, src],
            recv_sem=recv_sem.at[src], device_id=z_peer(way), device_id_type=MESH)

    def to_a(j):
        return sent(place(j), place(groups + j), groups + j, a_peer)

    def to_b(k):
        return sent(place(k), place(2 * groups + k), 2 * groups + k, b_peer)

    def to_core(k):
        return sent(place(k), place(k) + groups, 4 * groups + k, partner)

    def arrived(slot):
        sent(0, slot, 0, partner).wait_recv()

    def spread_out(k):
        to_a(k).start()
        to_b(k).start()
        to_core(k).start()

    def pass_on(z):
        arrived(place(groups + z))
        to_b(groups + z).start()
        to_core(groups + z).start()

    for way in (1, -1):
        @pl.when(follows(way))
        def _():
            to_z(g, way).start()
    spread_out(g)
    for d in range(1, groups + 1):
        if d < groups:
            for way in (1, -1):
                src = g - way * d

                @pl.when(inside(src))
                def _():
                    arrived(src)

                    @pl.when(follows(way))
                    def _():
                        to_z(src, way).start()

                    spread_out(src)
        for way in (1, -1) if d > 1 else (1,):
            src = g - way * (d - 1)

            @pl.when(inside(src))
            def _():
                pass_on(src)
    for load in loads:
        load.wait()

    def pair_copy(c):
        return pltpu.make_async_remote_copy(
            src_ref=contrib.at[pl.ds(c * span + groups, groups)], dst_ref=from_core.at[pl.ds(c * groups, groups)],
            send_sem=pair_send.at[c], recv_sem=pair_recv.at[c], device_id=partner, device_id_type=MESH)

    def b_copy(k):
        return pltpu.make_async_remote_copy(
            src_ref=contrib.at[place(2 * groups + k)], dst_ref=from_b.at[k],
            send_sem=ret_send.at[2 * groups + k], recv_sem=b_recv.at[k], device_id=b_peer, device_id_type=MESH)

    def a_copy(j):
        return pltpu.make_async_remote_copy(
            src_ref=contrib.at[place(groups + j)], dst_ref=from_a.at[j],
            send_sem=ret_send.at[groups + j], recv_sem=a_recv.at[j], device_id=a_peer, device_id_type=MESH)

    def z_copy(z, way):
        return pltpu.make_async_remote_copy(
            src_ref=contrib.at[z], dst_ref=from_z.at[(1 - way) // 2, z],
            send_sem=zr_send.at[(1 - way) // 2, z], recv_sem=z_recv.at[(1 - way) // 2, z],
            device_id=z_peer(way), device_id_type=MESH)

    upper = g // (groups // 2)

    def far_first(t):
        return t * upper + (groups - 1 - t) * (1 - upper)

    def back_to_b(c):
        pair_copy(c).wait_recv()

        def one(q, _):
            k = c * groups + far_first(q)
            s = place(k)
            contrib[s] = (contrib[s].astype(F32) + from_core[k].astype(F32)).astype(BF16)
            b_copy(k - 2 * groups).start()
            return 0

        lax.fori_loop(0, groups, one, 0)

    chunk_rows = span * cap
    chunk_toks = span * rows

    def chunk(c, meanwhile):
        block = tok.at[pl.ds(c * span, span)]
        tail = block[:, :, edge:].reshape(chunk_toks, 128).astype(F32)
        tail_lane = lax.broadcasted_iota(jnp.int32, (chunk_toks, 128), 1)
        rank1 = jnp.sum(jnp.where(tail_lane == me + own, tail, 0.0), axis=1, keepdims=True)
        slot = (lax.broadcasted_iota(jnp.int32, (chunk_toks, 1), 0) // rows * cap).astype(F32)
        where_to = jnp.where(rank1 > 0.5, slot + rank1 - 1.0, -1.0)
        column = lax.broadcasted_iota(jnp.int32, (chunk_toks, chunk_rows), 1).astype(F32)
        select = (where_to == column).astype(BF16)
        step = 512
        select_t = select.T
        for n in range(0, padded, step):
            size = min(step, padded - n)
            part = block[:, :, n:n + size].reshape(chunk_toks, size)
            picked[:, n:n + size] = jnp.dot(select_t, part, preferred_element_type=F32).astype(BF16)
        row_tail = picked[:, edge:].astype(F32)
        row_lane = lax.broadcasted_iota(jnp.int32, (chunk_rows, 128), 1)
        scale = jnp.sum(jnp.where(row_lane == me + (own + experts), row_tail, 0.0), axis=1, keepdims=True) * (1.0 / 32.0)

        def ffn(cols):
            x = picked[:, :width]
            gate = lax.dot_general(x, gate_w[cols, :], LAST, preferred_element_type=F32)
            up = lax.dot_general(x, up_w[cols, :], LAST, preferred_element_type=F32)
            hid[:, cols] = (gate * jax.nn.sigmoid(1.702 * gate) * (up + 1.0)).astype(BF16)

        whole, rest = tiles_of(half, FTILE)

        def ffn_step(n, _):
            meanwhile(n)
            ffn(pl.ds(pl.multiple_of(n * FTILE, FTILE), FTILE))
            return 0

        lax.fori_loop(0, whole, ffn_step, 0)
        if rest:
            ffn(pl.ds(whole * FTILE, rest))

        def down(cols, size):
            res = jnp.dot(hid[...], down_w[:, cols], preferred_element_type=F32) * scale
            spread = jnp.dot(select, res.astype(BF16), preferred_element_type=F32).astype(BF16)
            contrib[pl.ds(c * span, span), :, cols] = spread.reshape(span, rows, size)

        whole2, rest2 = tiles_of(width, DTILE)

        def down_step(n, _):
            down(pl.ds(pl.multiple_of(n * DTILE, DTILE), DTILE), DTILE)
            return 0

        lax.fori_loop(0, whole2, down_step, 0)
        if rest2:
            down(pl.ds(whole2 * DTILE, rest2), rest2)

    def stage(i, _):
        c = (4 - i) % 4

        @pl.when(i == 1)
        def _():
            def one(q, _):
                k = 2 * groups + q
                arrived(place(k))
                to_core(k).start()
                return 0

            lax.fori_loop(0, 2 * groups, one, 0)

        def got(q, _):
            arrived(c * span + groups + q)
            return 0

        lax.fori_loop(0, groups, got, 0)

        def meanwhile(n):
            @pl.when((n == PAUSE) & (i >= 2))
            def _():
                back_to_b((c + 1) % 4)

        chunk(c, meanwhile)
        pair_copy(c).start()
        return 0

    lax.fori_loop(0, 4, stage, 0)

    pair_copy(1).wait_recv()

    def a_step(t, _):
        j = far_first(t)
        b_copy(groups + j).wait_recv()
        s = place(groups + j)
        contrib[s] = (contrib[s].astype(F32) + from_core[groups + j].astype(F32)
                      + from_b[groups + j].astype(F32)).astype(BF16)
        a_copy(j).start()
        return 0

    lax.fori_loop(0, groups, a_step, 0)
    pair_copy(0).wait_recv()

    def gathered(z):
        return (contrib[z].astype(F32) + from_core[z].astype(F32)
                + from_b[z].astype(F32) + from_a[z].astype(F32))

    def z_step(t, _):
        z = far_first(t)
        b_copy(z).wait_recv()
        a_copy(z).wait_recv()
        acc[...] = gathered(z)
        for way in (1, -1):
            @pl.when((z - g) * way > 0)
            def _():
                @pl.when(follows(-way))
                def _():
                    z_copy(z, way).wait_recv()
                    acc[...] += from_z[(1 - way) // 2, z].astype(F32)

                contrib[z] = acc[...].astype(BF16)
                z_copy(z, way).start()

        return 0

    lax.fori_loop(0, groups, z_step, 0)
    acc[...] = gathered(g)
    for way in (1, -1):
        @pl.when(follows(-way))
        def _():
            z_copy(g, way).wait_recv()
            acc[...] += from_z[(1 - way) // 2, g].astype(F32)
    out[...] = acc[...].astype(BF16)

    for z in range(groups):
        for way in (1, -1):
            @pl.when(follows(way) & ((g - z) * way >= 0))
            def _():
                to_z(z, way).wait_send()

            @pl.when((z - g) * way > 0)
            def _():
                z_copy(z, way).wait_send()
        to_a(z).wait_send()
        a_copy(z).wait_send()
    for c in range(4):
        pair_copy(c).wait_send()
    for k in range(2 * groups):
        to_b(k).wait_send()
        b_copy(k).wait_send()
    for k in range(4 * groups):
        to_core(k).wait_send()


def gathered_plan(tokens, expert_ids, combine_int, gate_weight, up_weight, down_weight):
    experts = lax.axis_size("expert")
    rows, width = tokens.shape
    cap = 2 * expert_ids.shape[1] * rows // experts
    half = gate_weight.shape[2]
    groups = experts // 4
    padded = -(-width // 128) * 128
    span = 2 * groups
    vmem = pl.BlockSpec(memory_space=pltpu.VMEM)
    anywhere = pl.BlockSpec(memory_space=pl.ANY)
    dma = pltpu.SemaphoreType.DMA
    flops = 2 * 4 * span * cap * width * half * 3
    return pl.pallas_call(
        functools.partial(kernel, experts, cap),
        out_shape=jax.ShapeDtypeStruct((rows, width), BF16),
        in_specs=[vmem] * 3 + [anywhere] * 3,
        out_specs=vmem,
        scratch_shapes=[
            pltpu.VMEM((8 * groups, rows, padded), BF16),
            pltpu.VMEM((8 * groups, rows, width), BF16),
            pltpu.VMEM((4 * groups, rows, width), BF16),
            pltpu.VMEM((2 * groups, rows, width), BF16),
            pltpu.VMEM((groups, rows, width), BF16),
            pltpu.VMEM((2, groups, rows, width), BF16),
            pltpu.VMEM((rows, width), F32),
            pltpu.VMEM((span * cap, padded), BF16),
            pltpu.VMEM((span * cap, half), BF16),
            pltpu.VMEM((half, width), BF16),
            pltpu.VMEM((half, width), BF16),
            pltpu.VMEM((half, width), BF16),
            dma((3,)),
            dma((8 * groups,)),
            dma((8 * groups,)),
            dma((4,)),
            dma((4,)),
            dma((4 * groups,)),
            dma((2 * groups,)),
            dma((groups,)),
            dma((2, groups)),
            dma((2, groups)),
            dma((2, groups)),
        ],
        compiler_params=pltpu.CompilerParams(
            collective_id=0, has_side_effects=True, vmem_limit_bytes=67043328),
        cost_estimate=pl.CostEstimate(flops=flops, bytes_accessed=6 * width * half, transcendentals=0),
    )(tokens, expert_ids.T, combine_int.T, jnp.swapaxes(gate_weight, 1, 2), jnp.swapaxes(up_weight, 1, 2), down_weight)


def shards(tokens, expert_ids, *rest):
    experts = lax.axis_size("expert")
    rows, width = tokens.shape
    cap = 2 * expert_ids.shape[1] * rows // experts
    gathers = 2 * cap >= rows and experts % 4 == 0 and width % 128 + 2 * experts <= 128 and rows % 16 == 0 and width % 128 > 0
    plan = gathered_plan if gathers else padded_plan
    return plan(tokens, expert_ids, *rest)


def solution(mesh):
    return jax.shard_map(
        shards,
        mesh=mesh,
        in_specs=(
            P(("expert", "dp"), None),
            P(("expert", "dp"), None),
            P(("expert", "dp"), None),
            P("expert", None, "dp"),
            P("expert", None, "dp"),
            P("expert", "dp", None),
        ),
        out_specs=P(("expert", "dp"), None),
        check_vma=False,
    )
```
